512 devices in a mesh: gy: 32 (over x_hi, y, core), gx: 16 (over z, x_lo).
Axes of the slice: x: 4 (x_hi: 2, x_lo: 2; x = x_hi * 2 + x_lo), y: 8, z: 8, core: 2. Of those that a mesh axis runs over, the one named last changes fastest.
Arguments:
- patches: float32 [32, 16, 256, 256], P('gy', 'gx'), may hold values from -6 to 6
- w_query: float32 [2, 256, 256], replicated, may hold values from -0.375 to 0.375
- w_key: float32 [2, 256, 256], replicated, may hold values from -0.375 to 0.375
- w_value: float32 [2, 256, 256], replicated, may hold values from -0.375 to 0.375
- w_out: float32 [2, 256, 256], replicated, may hold values from -1.5 to 1.5
Outputs:
- embedded: float32 [32, 16, 256, 256], P('gy', 'gx')
The draws below stay inside these ranges and needn't reach their ends.
All inputs are finite; a program needn't handle non-finite values.
Results may differ from the reference program's by a relative error of at most 0.0003.
Values sent between devices are 32-bit elements; how exact they have to be, the bound alone decides.
A program may use at most 64 MiB of HBM per device.

```python
import jax
import jax.numpy as jnp
from jax import lax

D = 256
P_SIZE = 256
LAYERS = 2
TY = 32
TX = 16


def level_of(stream_key, extent, cuts, smallest, top_value):
    def one(position, blocks):
        draws = jax.random.uniform(jax.random.fold_in(jax.random.fold_in(stream_key, 6), position), (blocks,), jnp.float32, smallest / len(cuts), top_value / len(cuts))
        return jnp.repeat(jnp.exp(draws), extent[position] // blocks).reshape((-1,) + (1,) * (len(extent) - position - 1))

    gain = one(*cuts[0])
    for cut in cuts[1:]:
        gain = gain * one(*cut)
    return gain


def bell_draw(own_key, shape, spread, limit, pieces=(), held_as=jnp.bfloat16):
    drawn = spread * jax.random.normal(own_key, shape, jnp.float32)
    if pieces:
        drawn = drawn * level_of(own_key, shape, pieces, -0.22, 0.18)
    return jnp.clip(drawn, -limit, limit).astype(held_as)


def setup_inputs(seed: int = 0) -> dict:
    arg_keys = jax.random.split(jax.random.key(seed), 6)
    return {
        "patches": bell_draw(arg_keys[0], (TY, TX, P_SIZE, D), 1.0, 6.0, ((0, 32), (1, 16)), jnp.float32),
        "w_query": bell_draw(arg_keys[1], (LAYERS, D, D), D ** -0.5, 0.375, (), jnp.float32),
        "w_key": bell_draw(arg_keys[2], (LAYERS, D, D), D ** -0.5, 0.375, (), jnp.float32),
        "w_value": bell_draw(arg_keys[3], (LAYERS, D, D), D ** -0.5, 0.375, (), jnp.float32),
        "w_out": bell_draw(arg_keys[4], (LAYERS, D, D), (4.0 / D ** 0.5), 1.5, (), jnp.float32),
    }


EPSILON = 1e-06
SHARPNESS = 16.0
SCORE_SHIFT = 32.0

def unitize(rows):
    scale = lax.rsqrt(lax.optimization_barrier(jnp.mean(rows * rows, axis=-1, keepdims=True)) + EPSILON)
    return rows * scale * rows.shape[-1] ** (-0.5)

def project(field, matrix):
    return jnp.einsum('yxpd,de->yxpe', field, matrix, precision=lax.Precision.HIGHEST)

def layer_pass(field, wq_layer, wk_layer, wv_layer, wo_layer):
    query = unitize(project(field, wq_layer))
    keys = unitize(project(field, wk_layer))
    values = project(field, wv_layer)
    widths = ((1, 1), (1, 1), (0, 0), (0, 0))
    pad_query = jnp.pad(query, widths)
    pad_keys = jnp.pad(keys, widths)
    pad_values = jnp.pad(values, widths)
    present = jnp.pad(jnp.ones((TY, TX), jnp.float32), ((1, 1), (1, 1)))
    numer = jnp.zeros_like(values)
    total = jnp.zeros(values.shape[:3], values.dtype)
    for row_step in range(3):
        for col_step in range(3):
            far_query = pad_query[row_step:row_step + TY, col_step:col_step + TX]
            far_keys = pad_keys[row_step:row_step + TY, col_step:col_step + TX]
            far_values = pad_values[row_step:row_step + TY, col_step:col_step + TX]
            far_present = present[row_step:row_step + TY, col_step:col_step + TX]
            scores = jnp.einsum('yxpd,yxqd->yxpq', query, far_keys, precision=lax.Precision.HIGHEST)
            scores = scores + jnp.einsum('yxpd,yxqd->yxpq', keys, far_query, precision=lax.Precision.HIGHEST)
            weights = jnp.exp(SHARPNESS * scores - SCORE_SHIFT) * far_present[:, :, None, None].astype(scores.dtype)
            numer = numer + jnp.einsum('yxpq,yxqd->yxpd', weights, far_values, precision=lax.Precision.HIGHEST)
            total = total + lax.optimization_barrier(jnp.sum(weights, axis=-1))
    mixed = numer / total[..., None]
    return field + jax.nn.gelu(project(mixed, wo_layer), approximate=False)

def reference(patches, w_query, w_key, w_value, w_out):
    field = patches
    for layer in range(LAYERS):
        field = layer_pass(field, w_query[layer], w_key[layer], w_value[layer], w_out[layer])
    return field
```

```python
import functools

import jax
import jax.numpy as jnp
from jax import lax
from jax.experimental import pallas as pl
from jax.experimental.pallas import tpu as pltpu
from jax.sharding import PartitionSpec as P

D = 256
ROWS = 256
LAYERS = 2
CHUNKS = 2
CROWS = ROWS // CHUNKS
EPSILON = 1e-06
SCORE_SHIFT = 32.0
MESH = pl.DeviceIdType.MESH

OWN, NEAR, FAR = 0, 1, 2
NORTH, MID, SOUTH = 0, 1, 2

F32 = jnp.float32
BF16 = jnp.bfloat16


def split(x):
    hi = x.astype(BF16)
    return hi, (x - hi.astype(F32)).astype(BF16)


def dot(a, b, dims):
    return lax.dot_general(a, b, (dims, ((), ())), preferred_element_type=F32)


def dot3(a, b, dims):
    a_hi, a_lo = a
    b_hi, b_lo = b
    return dot(a_hi, b_hi, dims) + (dot(a_lo, b_hi, dims) + dot(a_hi, b_lo, dims))


NN = ((1,), (0,))
NT = ((1,), (1,))


def kernel(ny, nx, p_ref, wq_ref, wk_ref, wv_ref, wo_ref, o_ref,
           field, halo, norms, wq, wk, wv, wo, g_hi, g_lo, acc, tot,
           send_sem, recv_sem, load_sem):
    gy = lax.axis_index("gy")
    gx = lax.axis_index("gx")
    side = lax.rem(gx, 2)
    partner = gx + 1 - 2 * side
    onward = gx + 2 - 4 * side
    behind = gx - 2 + 4 * side
    has_onward = (onward >= 0) & (onward < nx)
    has_far = (behind >= 0) & (behind < nx)
    has_north = gy >= 1
    has_south = gy + 1 < ny

    loads = [pltpu.make_async_copy(p_ref, field.at[0], load_sem.at[0])]
    for n, (src, dst) in enumerate(((wq_ref, wq), (wk_ref, wk), (wv_ref, wv), (wo_ref, wo))):
        loads.append(pltpu.make_async_copy(src, dst, load_sem.at[n + 1]))
    for load in loads:
        load.start()

    barrier = pltpu.get_barrier_semaphore()

    def greet(y, x):
        pl.semaphore_signal(barrier, inc=1, device_id=(y, x), device_id_type=MESH)

    greet(gy, partner)
    pl.when(has_onward)(lambda: greet(gy, onward))
    pl.when(has_far)(lambda: greet(gy, behind))
    pl.when(has_north)(lambda: greet(gy - 1, gx))
    pl.when(has_south)(lambda: greet(gy + 1, gx))
    greetings = (1 + has_onward.astype(jnp.int32) + has_far.astype(jnp.int32)
                 + has_north.astype(jnp.int32) + has_south.astype(jnp.int32))
    loads[0].wait()
    pl.semaphore_wait(barrier, greetings)

    def rows(c):
        return pl.ds(c * CROWS, CROWS)

    def piece(layer, row, col, c, source=False):
        slot = row * 3 + col
        if c == CHUNKS:
            return norms.at[layer, slot]
        if source and row == MID and col == OWN:
            return field.at[layer, rows(c)]
        return halo.at[layer, slot, rows(c)]

    def sends():
        yield 0, OWN, MID, NEAR, (gy, partner), None
        yield 1, NEAR, MID, FAR, (gy, onward), has_onward
        for col in (OWN, NEAR, FAR):
            there = None if col != FAR else has_far
            yield 2 + col, col, SOUTH, col, (gy - 1, gx), has_north if there is None else has_north & there
            yield 5 + col, col, NORTH, col, (gy + 1, gx), has_south if there is None else has_south & there

    def copy(layer, send, c):
        kind, src_col, row, col, device, _ = send
        return pltpu.make_async_remote_copy(
            src_ref=piece(layer, MID, src_col, c, True),
            dst_ref=piece(layer, row, col, c),
            send_sem=send_sem.at[layer, kind, c],
            recv_sem=recv_sem.at[layer, row * 3 + col, c],
            device_id=device,
            device_id_type=MESH,
        )

    def guarded(condition, action):
        if condition is None:
            action()
        else:
            pl.when(condition)(action)

    plan = list(sends())

    def start(layer, src_col, c):
        for send in plan:
            if send[1] == src_col:
                guarded(send[5], lambda send=send: copy(layer, send, c).start())

    def arrival(layer, row, col, c):
        for send in plan:
            if send[2] == row and send[3] == col:
                copy(layer, send, c).wait_recv()

    def process(layer, row, col):
        slot = row * 3 + col
        tile = split(field[layer] if slot == 3 * MID + OWN else halo[layer, slot])
        n_rows = norms[layer, slot]
        both = dot3((g_hi[...], g_lo[...]), tile, NT)
        score = both[:ROWS] * n_rows[1:2] + both[ROWS:] * n_rows[0:1]
        weight = jnp.exp(score - SCORE_SHIFT)
        tot[...] += jnp.sum(weight, axis=1, keepdims=True)
        acc[...] += dot3(split(weight), tile, NN)

    def await_and_process(layer, row, col):
        def run():
            for c in range(CHUNKS + 1):
                arrival(layer, row, col, c)
            process(layer, row, col)
        conditions = {NORTH: has_north, SOUTH: has_south}[row]
        if col == FAR:
            conditions = conditions & has_far
        pl.when(conditions)(run)

    def layer_pass(layer, carry):
        for c in range(CHUNKS):
            start(layer, OWN, c)

        @pl.when(layer == 0)
        def _():
            for load in loads[1:]:
                load.wait()

        own = split(field[layer])
        wq_s = split(wq[layer])
        wk_s = split(wk[layer])
        query = dot3(own, wq_s, NN)
        keys = dot3(own, wk_s, NN)
        ones = jnp.ones((8, D), F32)

        def along_lanes(raw):
            total = lax.dot_general(ones, raw * raw, (NT, ((), ())),
                                    precision=lax.Precision.HIGHEST, preferred_element_type=F32)
            return lax.rsqrt(total * (1.0 / D) + EPSILON)

        first = lax.broadcasted_iota(jnp.int32, (8, ROWS), 0) == 0
        norms[layer, MID * 3 + OWN] = jnp.where(first, along_lanes(query), along_lanes(keys))
        start(layer, OWN, CHUNKS)

        def unitize(raw):
            scale = lax.rsqrt(jnp.mean(raw * raw, axis=-1, keepdims=True) + EPSILON)
            return raw * scale * D ** (-0.5)

        g1 = split(dot3(split(unitize(query)), wk_s, NT))
        g2 = split(dot3(split(unitize(keys)), wq_s, NT))
        g_hi[:ROWS] = g1[0]
        g_lo[:ROWS] = g1[1]
        g_hi[ROWS:] = g2[0]
        g_lo[ROWS:] = g2[1]
        acc[...] = jnp.zeros_like(acc)
        tot[...] = jnp.zeros_like(tot)
        process(layer, MID, OWN)

        for c in range(CHUNKS + 1):
            arrival(layer, MID, NEAR, c)
            start(layer, NEAR, c)
        process(layer, MID, NEAR)
        await_and_process(layer, NORTH, OWN)
        await_and_process(layer, SOUTH, OWN)

        @pl.when(has_far)
        def _():
            for c in range(CHUNKS + 1):
                arrival(layer, MID, FAR, c)
                start(layer, FAR, c)
            process(layer, MID, FAR)

        for col in (NEAR, FAR):
            for row in (NORTH, SOUTH):
                await_and_process(layer, row, col)

        mean = acc[...] * (1.0 / tot[...])
        mixed = dot3(split(mean), split(wv[layer]), NN)
        pre = dot3(split(mixed), split(wo[layer]), NN)
        field[layer + 1] = field[layer] + 0.5 * pre * (1.0 + lax.erf(pre * 0.5 ** 0.5))
        return carry

    lax.fori_loop(0, LAYERS, layer_pass, 0)
    o_ref[...] = field[LAYERS]

    def drain(layer, carry):
        for send in plan:
            for c in range(CHUNKS + 1):
                guarded(send[5], lambda send=send, c=c: copy(layer, send, c).wait_send())
        return carry

    lax.fori_loop(0, LAYERS, drain, 0)


def on_device(ny, nx, patches, w_query, w_key, w_value, w_out):
    any_space = pl.BlockSpec(memory_space=pl.ANY)
    weight = pltpu.VMEM((LAYERS, D, D), F32)
    out = pl.pallas_call(
        functools.partial(kernel, ny, nx),
        out_shape=jax.ShapeDtypeStruct((ROWS, D), F32),
        in_specs=[any_space] * 5,
        out_specs=pl.BlockSpec(memory_space=pltpu.VMEM),
        scratch_shapes=[
            pltpu.VMEM((LAYERS + 1, ROWS, D), F32),
            pltpu.VMEM((LAYERS, 9, ROWS, D), F32),
            pltpu.VMEM((LAYERS, 9, 8, ROWS), F32),
            weight, weight, weight, weight,
            pltpu.VMEM((2 * ROWS, D), BF16),
            pltpu.VMEM((2 * ROWS, D), BF16),
            pltpu.VMEM((ROWS, D), F32),
            pltpu.VMEM((ROWS, 1), F32),
            pltpu.SemaphoreType.DMA((LAYERS, 8, CHUNKS + 1)),
            pltpu.SemaphoreType.DMA((LAYERS, 9, CHUNKS + 1)),
            pltpu.SemaphoreType.DMA((5,)),
        ],
        compiler_params=pltpu.CompilerParams(
            collective_id=0, has_side_effects=True, vmem_limit_bytes=48 * 1024 * 1024
        ),
    )(patches[0, 0], w_query, w_key, w_value, w_out)
    return out[None, None]


def solution(mesh):
    in_specs = (P("gy", "gx", None, None), P(), P(), P(), P())
    out_specs = P("gy", "gx", None, None)
    return jax.shard_map(
        functools.partial(on_device, mesh.shape["gy"], mesh.shape["gx"]),
        mesh=mesh, in_specs=in_specs, out_specs=out_specs, check_vma=False
    )
```

```python
import functools

import jax
import jax.numpy as jnp
from jax import lax
from jax.experimental import pallas as pl
from jax.experimental.pallas import tpu as pltpu
from jax.sharding import PartitionSpec as P

D = 256
ROWS = 256
LAYERS = 2
CHUNKS = 4
CROWS = ROWS // CHUNKS
EPSILON = 1e-06
SCORE_SHIFT = 32.0
MESH = pl.DeviceIdType.MESH

OWN, NEAR, FAR = 0, 1, 2
PAIR, MID, AWAY = 0, 1, 2

F32 = jnp.float32
BF16 = jnp.bfloat16


def split(x):
    hi = x.astype(BF16)
    return hi, (x - hi.astype(F32)).astype(BF16)


def dot(a, b, dims):
    return lax.dot_general(a, b, (dims, ((), ())), preferred_element_type=F32)


def dot3(a, b, dims):
    a_hi, a_lo = a
    b_hi, b_lo = b
    return dot(a_hi, b_hi, dims) + (dot(a_lo, b_hi, dims) + dot(a_hi, b_lo, dims))


NN = ((1,), (0,))
NT = ((1,), (1,))


def kernel(ny, nx, p_ref, wq_ref, wk_ref, wv_ref, wo_ref, o_ref,
           field, halo, norms, wq, wk, wv, wo, g_hi, g_lo, acc, tot,
           send_sem, recv_sem, load_sem):
    gy = lax.axis_index("gy")
    gx = lax.axis_index("gx")
    side = lax.rem(gx, 2)
    partner = gx + 1 - 2 * side
    onward = gx + 2 - 4 * side
    behind = gx - 2 + 4 * side
    has_onward = (onward >= 0) & (onward < nx)
    has_far = (behind >= 0) & (behind < nx)
    odd = lax.rem(gy, 2)
    pair_y = gy + 1 - 2 * odd
    away_y = gy - 1 + 2 * odd
    seam = (gy == ny // 2) | (gy == ny // 2 - 1)
    has_away = (away_y >= 0) & (away_y < ny)

    loads = [pltpu.make_async_copy(p_ref, field.at[0], load_sem.at[0])]
    for n, (src, dst) in enumerate(((wq_ref, wq), (wk_ref, wk), (wv_ref, wv), (wo_ref, wo))):
        loads.append(pltpu.make_async_copy(src, dst, load_sem.at[n + 1]))
    for load in loads:
        load.start()

    barrier = pltpu.get_barrier_semaphore()

    def greet(y, x):
        pl.semaphore_signal(barrier, inc=1, device_id=(y, x), device_id_type=MESH)

    greet(gy, partner)
    pl.when(has_onward)(lambda: greet(gy, onward))
    pl.when(has_far)(lambda: greet(gy, behind))
    greet(pair_y, gx)
    pl.when(has_away)(lambda: greet(away_y, gx))
    greetings = (2 + has_onward.astype(jnp.int32) + has_far.astype(jnp.int32)
                 + has_away.astype(jnp.int32))
    loads[0].wait()
    pl.semaphore_wait(barrier, greetings)

    def rows(c):
        return pl.ds(c * CROWS, CROWS)

    def piece(layer, row, col, c, source=False):
        slot = row * 3 + col
        if c == CHUNKS:
            return norms.at[layer, slot]
        if source and row == MID and col == OWN:
            return field.at[layer, rows(c)]
        return halo.at[layer, slot, rows(c)]

    plain = has_away & jnp.logical_not(seam)
    plan = [
        (5, (MID, OWN), (AWAY, OWN), (away_y, gx), has_away),
        (0, (MID, OWN), (MID, NEAR), (gy, partner), None),
        (2, (MID, OWN), (PAIR, OWN), (pair_y, gx), None),
        (1, (MID, NEAR), (MID, FAR), (gy, onward), has_onward),
        (6, (MID, NEAR), (AWAY, NEAR), (away_y, gx), plain),
        (3, (MID, NEAR), (PAIR, NEAR), (pair_y, gx), None),
        (7, (MID, FAR), (AWAY, FAR), (away_y, gx), plain & has_far),
        (4, (MID, FAR), (PAIR, FAR), (pair_y, gx), has_far),
        (8, (AWAY, OWN), (AWAY, NEAR), (gy, partner), seam),
        (9, (AWAY, NEAR), (AWAY, FAR), (gy, onward), seam & has_onward),
    ]

    def copy(layer, send, c):
        kind, source, target, device, _ = send
        return pltpu.make_async_remote_copy(
            src_ref=piece(layer, *source, c, True),
            dst_ref=piece(layer, *target, c),
            send_sem=send_sem.at[layer, kind, c],
            recv_sem=recv_sem.at[layer, target[0] * 3 + target[1], c],
            device_id=device,
            device_id_type=MESH,
        )

    def guarded(condition, action):
        if condition is None:
            action()
        else:
            pl.when(condition)(action)

    def start(layer, source, chunks):
        for send in plan:
            if send[1] == source:
                def run(send=send):
                    for c in chunks:
                        copy(layer, send, c).start()
                guarded(send[4], run)

    def arrival(layer, row, col, c):
        there = piece(layer, row, col, c)
        pltpu.make_async_remote_copy(
            src_ref=there, dst_ref=there, send_sem=send_sem.at[layer, 0, c],
            recv_sem=recv_sem.at[layer, row * 3 + col, c],
            device_id=(gy, partner), device_id_type=MESH,
        ).wait_recv()

    def process(layer, row, col):
        slot = row * 3 + col
        tile = split(field[layer] if slot == 3 * MID + OWN else halo[layer, slot])
        n_rows = norms[layer, slot]
        both = dot3((g_hi[...], g_lo[...]), tile, NT)
        score = both[:ROWS] * n_rows[1:2] + both[ROWS:] * n_rows[0:1]
        weight = jnp.exp(score - SCORE_SHIFT)
        tot[...] += jnp.sum(weight, axis=1, keepdims=True)
        acc[...] += dot3(split(weight), tile, NN)

    def take(layer, row, col):
        def run():
            for c in range(CHUNKS + 1):
                arrival(layer, row, col, c)
                start(layer, (row, col), [c])
            process(layer, row, col)
        condition = has_away if row == AWAY else None
        if col == FAR:
            condition = has_far if condition is None else condition & has_far
        guarded(condition, run)

    def layer_pass(layer, carry):
        start(layer, (MID, OWN), range(CHUNKS))

        @pl.when(layer == 0)
        def _():
            for load in loads[1:]:
                load.wait()

        own = split(field[layer])
        wq_s = split(wq[layer])
        wk_s = split(wk[layer])
        query = dot3(own, wq_s, NN)
        keys = dot3(own, wk_s, NN)
        ones = jnp.ones((8, D), F32)

        def along_lanes(raw):
            total = lax.dot_general(ones, raw * raw, (NT, ((), ())),
                                    precision=lax.Precision.HIGHEST, preferred_element_type=F32)
            return lax.rsqrt(total * (1.0 / D) + EPSILON)

        first = lax.broadcasted_iota(jnp.int32, (8, ROWS), 0) == 0
        norms[layer, MID * 3 + OWN] = jnp.where(first, along_lanes(query), along_lanes(keys))
        start(layer, (MID, OWN), [CHUNKS])

        def unitize(raw):
            scale = lax.rsqrt(jnp.mean(raw * raw, axis=-1, keepdims=True) + EPSILON)
            return raw * scale * D ** (-0.5)

        g1 = split(dot3(split(unitize(query)), wk_s, NT))
        g2 = split(dot3(split(unitize(keys)), wq_s, NT))
        g_hi[:ROWS] = g1[0]
        g_lo[:ROWS] = g1[1]
        g_hi[ROWS:] = g2[0]
        g_lo[ROWS:] = g2[1]
        acc[...] = jnp.zeros_like(acc)
        tot[...] = jnp.zeros_like(tot)
        process(layer, MID, OWN)

        take(layer, MID, NEAR)
        take(layer, PAIR, OWN)
        take(layer, MID, FAR)
        take(layer, AWAY, OWN)
        take(layer, PAIR, NEAR)
        take(layer, AWAY, NEAR)
        take(layer, PAIR, FAR)
        take(layer, AWAY, FAR)

        mean = acc[...] * (1.0 / tot[...])
        mixed = dot3(split(mean), split(wv[layer]), NN)
        pre = dot3(split(mixed), split(wo[layer]), NN)
        field[layer + 1] = field[layer] + 0.5 * pre * (1.0 + lax.erf(pre * 0.5 ** 0.5))
        return carry

    lax.fori_loop(0, LAYERS, layer_pass, 0)
    o_ref[...] = field[LAYERS]

    def drain(layer, carry):
        for send in plan:
            def run(send=send):
                for c in range(CHUNKS + 1):
                    copy(layer, send, c).wait_send()
            guarded(send[4], run)
        return carry

    lax.fori_loop(0, LAYERS, drain, 0)


def on_device(ny, nx, patches, w_query, w_key, w_value, w_out):
    in_hbm = pl.BlockSpec(memory_space=pltpu.HBM)
    weight = pltpu.VMEM((LAYERS, D, D), F32)
    out = pl.pallas_call(
        functools.partial(kernel, ny, nx),
        out_shape=jax.ShapeDtypeStruct((ROWS, D), F32),
        in_specs=[in_hbm] * 5,
        out_specs=pl.BlockSpec(memory_space=pltpu.VMEM),
        scratch_shapes=[
            pltpu.VMEM((LAYERS + 1, ROWS, D), F32),
            pltpu.VMEM((LAYERS, 9, ROWS, D), F32),
            pltpu.VMEM((LAYERS, 9, 8, ROWS), F32),
            weight, weight, weight, weight,
            pltpu.VMEM((2 * ROWS, D), BF16),
            pltpu.VMEM((2 * ROWS, D), BF16),
            pltpu.VMEM((ROWS, D), F32),
            pltpu.VMEM((ROWS, 1), F32),
            pltpu.SemaphoreType.DMA((LAYERS, 10, CHUNKS + 1)),
            pltpu.SemaphoreType.DMA((LAYERS, 9, CHUNKS + 1)),
            pltpu.SemaphoreType.DMA((5,)),
        ],
        compiler_params=pltpu.CompilerParams(
            collective_id=0, has_side_effects=True, vmem_limit_bytes=67043328
        ),
    )(patches[0, 0], w_query, w_key, w_value, w_out)
    return out[None, None]


def solution(mesh):
    in_specs = (P("gy", "gx", None, None), P(), P(), P(), P())
    out_specs = P("gy", "gx", None, None)
    return jax.shard_map(
        functools.partial(on_device, mesh.shape["gy"], mesh.shape["gx"]),
        mesh=mesh, in_specs=in_specs, out_specs=out_specs, check_vma=False
    )
```

```python
import functools

import jax
import jax.numpy as jnp
from jax import lax
from jax.experimental import pallas as pl
from jax.experimental.pallas import tpu as pltpu
from jax.sharding import PartitionSpec as P

D = 256
ROWS = 256
LAYERS = 2
CHUNKS = 4
CROWS = ROWS // CHUNKS
EPSILON = 1e-06
SCORE_SHIFT = 32.0
MESH = pl.DeviceIdType.MESH

OWN, NEAR, FAR = 0, 1, 2
PAIR, MID, AWAY = 0, 1, 2

F32 = jnp.float32
BF16 = jnp.bfloat16


def split(x):
    hi = x.astype(BF16)
    return hi, (x - hi.astype(F32)).astype(BF16)


def dot(a, b, dims):
    return lax.dot_general(a, b, (dims, ((), ())), preferred_element_type=F32)


def dot3(a, b, dims):
    a_hi, a_lo = a
    b_hi, b_lo = b
    return dot(a_hi, b_hi, dims) + (dot(a_lo, b_hi, dims) + dot(a_hi, b_lo, dims))


NN = ((1,), (0,))
NT = ((1,), (1,))


def kernel(ny, nx, p_ref, wq_ref, wk_ref, wv_ref, wo_ref, o_ref,
           field, halo, norms, wq, wk, wv, wo, g_hi, g_lo, acc, tot,
           send_sem, recv_sem, load_sem):
    gy = lax.axis_index("gy")
    gx = lax.axis_index("gx")
    side = lax.rem(gx, 2)
    partner = gx + 1 - 2 * side
    onward = gx + 2 - 4 * side
    behind = gx - 2 + 4 * side
    has_onward = (onward >= 0) & (onward < nx)
    has_far = (behind >= 0) & (behind < nx)
    odd = lax.rem(gy, 2)
    pair_y = gy + 1 - 2 * odd
    away_y = gy - 1 + 2 * odd
    seam = (gy == ny // 2) | (gy == ny // 2 - 1)
    has_away = (away_y >= 0) & (away_y < ny)

    loads = [pltpu.make_async_copy(p_ref, field.at[0], load_sem.at[0])]
    for n, (src, dst) in enumerate(((wq_ref, wq), (wk_ref, wk), (wv_ref, wv), (wo_ref, wo))):
        loads.append(pltpu.make_async_copy(src, dst, load_sem.at[n + 1]))
    loads[0].start()

    barrier = pltpu.get_barrier_semaphore()

    def greet(y, x):
        pl.semaphore_signal(barrier, inc=1, device_id=(y, x), device_id_type=MESH)

    greet(gy, partner)
    pl.when(has_onward)(lambda: greet(gy, onward))
    pl.when(has_far)(lambda: greet(gy, behind))
    greet(pair_y, gx)
    pl.when(has_away)(lambda: greet(away_y, gx))
    greetings = (2 + has_onward.astype(jnp.int32) + has_far.astype(jnp.int32)
                 + has_away.astype(jnp.int32))
    loads[0].wait()
    for load in loads[1:]:
        load.start()
    pl.semaphore_wait(barrier, greetings)

    def rows(c):
        return pl.ds(c * CROWS, CROWS)

    def piece(layer, row, col, c, source=False):
        slot = row * 3 + col
        if c == CHUNKS:
            return norms.at[layer, slot]
        if source and row == MID and col == OWN:
            return field.at[layer, rows(c)]
        return halo.at[layer, slot, rows(c)]

    plain = has_away & jnp.logical_not(seam)
    plan = [
        (5, (MID, OWN), (AWAY, OWN), (away_y, gx), has_away),
        (0, (MID, OWN), (MID, NEAR), (gy, partner), None),
        (2, (MID, OWN), (PAIR, OWN), (pair_y, gx), None),
        (1, (MID, NEAR), (MID, FAR), (gy, onward), has_onward),
        (6, (MID, NEAR), (AWAY, NEAR), (away_y, gx), plain),
        (3, (MID, NEAR), (PAIR, NEAR), (pair_y, gx), None),
        (7, (MID, FAR), (AWAY, FAR), (away_y, gx), plain & has_far),
        (4, (MID, FAR), (PAIR, FAR), (pair_y, gx), has_far),
        (8, (AWAY, OWN), (AWAY, NEAR), (gy, partner), seam),
        (9, (AWAY, NEAR), (AWAY, FAR), (gy, onward), seam & has_onward),
    ]

    def copy(layer, send, c):
        kind, source, target, device, _ = send
        return pltpu.make_async_remote_copy(
            src_ref=piece(layer, *source, c, True),
            dst_ref=piece(layer, *target, c),
            send_sem=send_sem.at[layer, kind, c],
            recv_sem=recv_sem.at[layer, target[0] * 3 + target[1], c],
            device_id=device,
            device_id_type=MESH,
        )

    def guarded(condition, action):
        if condition is None:
            action()
        else:
            pl.when(condition)(action)

    def start(layer, source, chunks):
        for send in plan:
            if send[1] == source:
                def run(send=send):
                    for c in chunks:
                        copy(layer, send, c).start()
                guarded(send[4], run)

    def arrival(layer, row, col, c):
        there = piece(layer, row, col, c)
        pltpu.make_async_remote_copy(
            src_ref=there, dst_ref=there, send_sem=send_sem.at[layer, 0, c],
            recv_sem=recv_sem.at[layer, row * 3 + col, c],
            device_id=(gy, partner), device_id_type=MESH,
        ).wait_recv()

    def process(layer, row, col):
        slot = row * 3 + col
        tile = split(field[layer] if slot == 3 * MID + OWN else halo[layer, slot])
        n_rows = norms[layer, slot]
        both = dot3((g_hi[...], g_lo[...]), tile, NT)
        score = both[:ROWS] * n_rows[1:2] + both[ROWS:] * n_rows[0:1]
        weight = jnp.exp(score - SCORE_SHIFT)
        tot[...] += jnp.sum(weight, axis=1, keepdims=True)
        acc[...] += dot3(split(weight), tile, NN)

    def take(layer, row, col):
        def run():
            for c in range(CHUNKS + 1):
                arrival(layer, row, col, c)
                start(layer, (row, col), [c])
            process(layer, row, col)
        condition = has_away if row == AWAY else None
        if col == FAR:
            condition = has_far if condition is None else condition & has_far
        guarded(condition, run)

    def layer_pass(layer, carry):
        start(layer, (MID, OWN), range(CHUNKS))

        @pl.when(layer == 0)
        def _():
            for load in loads[1:]:
                load.wait()

        own = split(field[layer])
        wq_s = split(wq[layer])
        wk_s = split(wk[layer])
        query = dot3(own, wq_s, NN)
        keys = dot3(own, wk_s, NN)
        ones = jnp.ones((8, D), F32)

        def along_lanes(raw):
            total = lax.dot_general(ones, raw * raw, (NT, ((), ())),
                                    precision=lax.Precision.HIGHEST, preferred_element_type=F32)
            return lax.rsqrt(total * (1.0 / D) + EPSILON)

        first = lax.broadcasted_iota(jnp.int32, (8, ROWS), 0) == 0
        norms[layer, MID * 3 + OWN] = jnp.where(first, along_lanes(query), along_lanes(keys))
        start(layer, (MID, OWN), [CHUNKS])

        def unitize(raw):
            scale = lax.rsqrt(jnp.mean(raw * raw, axis=-1, keepdims=True) + EPSILON)
            return raw * scale * D ** (-0.5)

        g1 = split(dot3(split(unitize(query)), wk_s, NT))
        g2 = split(dot3(split(unitize(keys)), wq_s, NT))
        g_hi[:ROWS] = g1[0]
        g_lo[:ROWS] = g1[1]
        g_hi[ROWS:] = g2[0]
        g_lo[ROWS:] = g2[1]
        acc[...] = jnp.zeros_like(acc)
        tot[...] = jnp.zeros_like(tot)
        process(layer, MID, OWN)

        take(layer, MID, NEAR)
        take(layer, PAIR, OWN)
        take(layer, MID, FAR)
        take(layer, PAIR, NEAR)
        take(layer, AWAY, OWN)
        take(layer, AWAY, NEAR)
        take(layer, PAIR, FAR)
        take(layer, AWAY, FAR)

        mean = acc[...] * (1.0 / tot[...])
        mixed = dot3(split(mean), split(wv[layer]), NN)
        pre = dot3(split(mixed), split(wo[layer]), NN)
        field[layer + 1] = field[layer] + 0.5 * pre * (1.0 + lax.erf(pre * 0.5 ** 0.5))
        return carry

    lax.fori_loop(0, LAYERS, layer_pass, 0)
    o_ref[...] = field[LAYERS]

    def drain(layer, carry):
        for send in plan:
            def run(send=send):
                for c in range(CHUNKS + 1):
                    copy(layer, send, c).wait_send()
            guarded(send[4], run)
        return carry

    lax.fori_loop(0, LAYERS, drain, 0)


def on_device(ny, nx, patches, w_query, w_key, w_value, w_out):
    in_hbm = pl.BlockSpec(memory_space=pltpu.HBM)
    weight = pltpu.VMEM((LAYERS, D, D), F32)
    out = pl.pallas_call(
        functools.partial(kernel, ny, nx),
        out_shape=jax.ShapeDtypeStruct((ROWS, D), F32),
        in_specs=[in_hbm] * 5,
        out_specs=pl.BlockSpec(memory_space=pltpu.VMEM),
        scratch_shapes=[
            pltpu.VMEM((LAYERS + 1, ROWS, D), F32),
            pltpu.VMEM((LAYERS, 9, ROWS, D), F32),
            pltpu.VMEM((LAYERS, 9, 8, ROWS), F32),
            weight, weight, weight, weight,
            pltpu.VMEM((2 * ROWS, D), BF16),
            pltpu.VMEM((2 * ROWS, D), BF16),
            pltpu.VMEM((ROWS, D), F32),
            pltpu.VMEM((ROWS, 1), F32),
            pltpu.SemaphoreType.DMA((LAYERS, 10, CHUNKS + 1)),
            pltpu.SemaphoreType.DMA((LAYERS, 9, CHUNKS + 1)),
            pltpu.SemaphoreType.DMA((5,)),
        ],
        compiler_params=pltpu.CompilerParams(
            collective_id=0, has_side_effects=True, vmem_limit_bytes=67043328
        ),
    )(patches[0, 0], w_query, w_key, w_value, w_out)
    return out[None, None]


def solution(mesh):
    in_specs = (P("gy", "gx", None, None), P(), P(), P(), P())
    out_specs = P("gy", "gx", None, None)
    return jax.shard_map(
        functools.partial(on_device, mesh.shape["gy"], mesh.shape["gx"]),
        mesh=mesh, in_specs=in_specs, out_specs=out_specs, check_vma=False
    )
```
